32 devices in a mesh: ctx: 8 (over z, x), head: 4 (over y, core).
Axes of the slice: x: 2, y: 2, z: 4, core: 2. Of those that a mesh axis runs over, the one named last changes fastest.
Arguments:
- queries: bfloat16 [1024, 8192], P('ctx', 'head'), may hold values from -110 to 110
- key_heads: bfloat16 [1024, 1024], P('ctx'), may hold values from -4.61 to 4.61
- value_heads: bfloat16 [1024, 1024], P('ctx'), may hold values from -6 to 6
- span_order: int32 [16], replicated, may hold values from 0 to 15, each once
- block_mask: int32 [16, 16], replicated, may hold values 0 or 1
- mamba_in: bfloat16 [1024, 16384], P('ctx', 'head'), may hold values from -6 to 6
- gate_in: bfloat16 [1024, 16384], P('ctx', 'head'), may hold values from -6 to 6
- conv_weight: float32 [4, 16384], P(None, 'head'), may hold values from -3 to 3
- conv_bias: float32 [16384], P('head'), may hold values from -3 to 3
- low_weight: bfloat16 [16384, 512], P('head'), may hold values from -0.046875 to 0.046875
- bc_weight: bfloat16 [16384, 32], P('head'), may hold values from -0.046875 to 0.046875
- low_gain: float32 [512], replicated, may hold values from 0.1 to 1.9
- dt_weight: bfloat16 [512, 16384], P(None, 'head'), may hold values from -0.25 to 0.25
- dt_bias: float32 [16384], P('head'), may hold values from -7 to -2
- rate_log: float32 [16384, 16], P('head'), may hold values from -3 to 2.77
- skip_gain: float32 [16384], P('head'), may hold values from 0.5 to 1.5
Outputs:
- attn_out: bfloat16 [1024, 8192], P('ctx', 'head')
- mamba_out: bfloat16 [1024, 16384], P('ctx', 'head')
The draws below stay inside these ranges and needn't reach their ends.
Inputs may be any that keep to these rules, and one draw needn't show every extreme that they name: `span_order`: each of the 16 span numbers stands in exactly one slot.
All inputs are finite; a program needn't handle non-finite values.
Results may differ from the reference program's by a relative error of at most 0.013.
Values may be sent and summed in bfloat16 or wider, within the bound.
No kernel may reach another device: no remote copies, remote signals or barrier semaphores. Data moves between devices by JAX's collectives and lax.ppermute only.
A program may use at most 192 MiB of HBM per device.

```python
import jax
import jax.numpy as jnp
from jax import lax

QHEADS = 64
KVHEADS = 8
HD = 128
INNER = 16384
STATE = 16
DTRANK = 512
CONV = 4
HALF = 64
NSPAN = 16
TOKENS = 1024


def query_key_pair(key):
    base_key = jax.random.fold_in(key, 7001)
    key_draw, query_draw = jax.random.split(base_key)
    key_vals = jax.random.truncated_normal(key_draw, -4.5, 4.5, (TOKENS, KVHEADS * HD), jnp.float32)
    query_vals = jax.random.truncated_normal(query_draw, -4.5, 4.5, (TOKENS, QHEADS * HD), jnp.float32)
    return (query_vals, key_vals)


def draw_queries(key, part):
    return query_key_pair(key)[0].astype(jnp.bfloat16)


def draw_key_heads(key, part):
    return query_key_pair(key)[1].astype(jnp.bfloat16)


def touch_ends(values, rng, smallest, high):
    longest = values.shape.index(max(values.shape))
    spots = []
    for shift in (0, 1):
        where = [jax.random.randint(jax.random.fold_in(rng, axis), (), 0, length) for axis, length in enumerate(values.shape)]
        where[longest] = (where[longest] + shift) % values.shape[longest]
        spots.append(tuple(where))
    return values.at[spots[0]].set(smallest).at[spots[1]].set(high)


def levels(rng, extent, pieces, least, largest):
    def one(position, blocks):
        draws = jax.random.uniform(jax.random.fold_in(jax.random.fold_in(rng, 6), position), (blocks,), jnp.float32, least / len(pieces), largest / len(pieces))
        return jnp.repeat(jnp.exp(draws), extent[position] // blocks).reshape((-1,) + (1,) * (len(extent) - position - 1))

    loudness = one(*pieces[0])
    for cut in pieces[1:]:
        loudness = loudness * one(*cut)
    return loudness


def bell_draw(own_key, dims, scale, reach, pieces=(), kind=jnp.bfloat16):
    entries = scale * jax.random.normal(own_key, dims, jnp.float32)
    if pieces:
        entries = entries * levels(own_key, dims, pieces, -0.22, 0.18)
    return jnp.clip(entries, -reach, reach).astype(kind)


def setup_inputs(seed: int = 0) -> dict:
    splits = jax.random.split(jax.random.key(seed), 17)
    return {
        "queries": draw_queries(jax.random.fold_in(splits[16], 71), 0),
        "key_heads": draw_key_heads(jax.random.fold_in(splits[16], 71), 0),
        "value_heads": bell_draw(splits[2], (TOKENS, KVHEADS * HD), 1.0, 6.0, ((0, 8),)),
        "span_order": jax.random.permutation(splits[3], NSPAN).astype(jnp.int32),
        "block_mask": touch_ends((jax.random.randint(splits[4], (NSPAN, NSPAN), 0, 4) < 3).astype(jnp.int32), jax.random.fold_in(splits[4], 1), 0, 1),
        "mamba_in": bell_draw(splits[5], (TOKENS, INNER), 1.0, 6.0, ((0, 8), (1, 4))),
        "gate_in": bell_draw(splits[6], (TOKENS, INNER), 1.0, 6.0, ((0, 8), (1, 4))),
        "conv_weight": bell_draw(splits[7], (CONV, INNER), 0.5, 3.0, ((1, 4),), jnp.float32),
        "conv_bias": bell_draw(splits[8], (INNER,), 0.5, 3.0, ((0, 4),), jnp.float32),
        "low_weight": bell_draw(splits[9], (INNER, DTRANK), INNER ** -0.5, 0.046875, ((0, 4),)),
        "bc_weight": bell_draw(splits[10], (INNER, 2 * STATE), INNER ** -0.5, 0.046875, ((0, 4),)),
        "low_gain": jnp.clip(1.0 + 0.18 * jax.random.normal(splits[11], (DTRANK,), jnp.float32), 0.1, 1.9),
        "dt_weight": bell_draw(splits[12], (DTRANK, INNER), DTRANK ** -0.5, 0.25, ((1, 4),)),
        "dt_bias": jnp.clip(-7.0 + 5.0 * jax.random.uniform(splits[13], (INNER,), jnp.float32) ** levels(splits[13], (INNER,), ((0, 4),), -0.2, 0.2), -7.0, -2.0),
        "rate_log": jnp.clip(-3.0 + 5.77 * jax.random.uniform(splits[14], (INNER, STATE), jnp.float32) ** levels(splits[14], (INNER, STATE), ((0, 4),), -0.2, 0.2), -3.0, 2.77),
        "skip_gain": jnp.clip(0.5 + 1.0 * jax.random.uniform(splits[15], (INNER,), jnp.float32) ** levels(splits[15], (INNER,), ((0, 4),), -0.2, 0.2), 0.5, 1.5),
    }


def attention_ref(queries, key_heads, value_heads, span_order, block_mask):
    row_ids = jnp.arange(TOKENS, dtype=jnp.int32)
    span_ids = span_order[row_ids // HALF]
    positions = span_ids * HALF + row_ids % HALF
    granted = block_mask[span_ids[:, None], span_ids[None, :]] == 1
    visible = (granted | (span_ids[:, None] == span_ids[None, :])) & (positions[None, :] <= positions[:, None])
    group_size = QHEADS // KVHEADS

    def one_head(head_index):
        query_part = lax.dynamic_slice_in_dim(queries, head_index * HD, HD, 1).astype(jnp.float32)
        key_part = lax.dynamic_slice_in_dim(key_heads, head_index // group_size * HD, HD, 1).astype(jnp.float32)
        value_part = lax.dynamic_slice_in_dim(value_heads, head_index // group_size * HD, HD, 1).astype(jnp.float32)
        scores = jnp.dot(query_part, key_part.T, preferred_element_type=jnp.float32) * HD ** (-0.5)
        scores = jnp.where(visible, scores, -jnp.inf)
        highest = lax.optimization_barrier(jnp.max(scores, axis=1, keepdims=True))
        weights = jnp.where(visible, jnp.exp(scores - highest), 0.0)
        totals = lax.optimization_barrier(jnp.sum(weights, axis=1, keepdims=True))
        rounded = lax.optimization_barrier(weights.astype(jnp.bfloat16)).astype(jnp.float32)
        return jnp.dot(rounded, value_part, preferred_element_type=jnp.float32) / totals
    heads_out = lax.map(one_head, jnp.arange(QHEADS, dtype=jnp.int32))
    return heads_out.transpose(1, 0, 2).reshape(TOKENS, QHEADS * HD).astype(jnp.bfloat16)

def mamba_ref(mamba_in, gate_in, conv_weight, conv_bias, low_weight, bc_weight, low_gain, dt_weight, dt_bias, rate_log, skip_gain):
    padded = jnp.concatenate([jnp.zeros((CONV - 1, INNER), jnp.float32), mamba_in.astype(jnp.float32)], axis=0)
    mixed = conv_bias[None, :] + sum((conv_weight[offset][None, :] * padded[offset:offset + TOKENS] for offset in range(CONV)))
    act_bf = jax.nn.silu(mixed).astype(jnp.bfloat16)
    act_wide = lax.optimization_barrier(act_bf).astype(jnp.float32)
    low_sum = jnp.dot(act_wide, low_weight.astype(jnp.float32), preferred_element_type=jnp.float32)
    bc_sum = jnp.dot(act_wide, bc_weight.astype(jnp.float32), preferred_element_type=jnp.float32)
    scale_inv = lax.rsqrt(lax.optimization_barrier(jnp.mean(low_sum * low_sum, axis=1, keepdims=True)) + 1e-06)
    normed = (low_sum * scale_inv * low_gain[None, :]).astype(jnp.bfloat16)
    normed_wide = lax.optimization_barrier(normed).astype(jnp.float32)
    step_dt = jax.nn.softplus(jnp.dot(normed_wide, dt_weight.astype(jnp.float32), preferred_element_type=jnp.float32) + dt_bias[None, :])
    rate_table = -jnp.exp(rate_log)

    def advance(state, packed):
        dt_row, in_row, bc_row = packed
        state = jnp.exp(dt_row[:, None] * rate_table) * state + (dt_row * in_row)[:, None] * bc_row[None, :STATE]
        return (state, lax.optimization_barrier(jnp.sum(state * bc_row[None, STATE:], axis=1)))
    _, outputs = lax.scan(advance, jnp.zeros((INNER, STATE), jnp.float32), (step_dt, act_wide, bc_sum))
    result = outputs + skip_gain[None, :] * act_wide
    return (result * jax.nn.silu(gate_in.astype(jnp.float32))).astype(jnp.bfloat16)

def reference(queries, key_heads, value_heads, span_order, block_mask, mamba_in, gate_in, conv_weight, conv_bias, low_weight, bc_weight, low_gain, dt_weight, dt_bias, rate_log, skip_gain):
    attn_out = attention_ref(queries, key_heads, value_heads, span_order, block_mask)
    mamba_out = mamba_ref(mamba_in, gate_in, conv_weight, conv_bias, low_weight, bc_weight, low_gain, dt_weight, dt_bias, rate_log, skip_gain)
    return (attn_out, mamba_out)
```

```python
import functools

import jax
import jax.numpy as jnp
from jax import lax
from jax.experimental import pallas as pl
from jax.experimental.pallas import tpu as pltpu
from jax.sharding import PartitionSpec as P

HD = 128
STATE = 16
CONV = 4
RIM = 8
LANES = 128
TOKEN_BLOCK = 16
LOG2E = 1.4426950408889634
NEG_FILL = -1e30
F32 = jnp.float32
BF16 = jnp.bfloat16


def swap(value, axis, step):
    count = lax.axis_size(axis)
    return lax.ppermute(value, axis, [(i, i ^ step) for i in range(count)])


def bits_of(count):
    steps = []
    while 2 ** len(steps) < count:
        steps.append(2 ** len(steps))
    return steps


def cost(flops, moved, exps=0):
    return pl.CostEstimate(flops=flops, bytes_accessed=moved, transcendentals=exps)


def attention_body(
    place, span_order, block_mask, q_ref, ka_ref, kb_ref, va_ref, vb_ref, out_ref, bias, *, order, heads
):
    half = q_ref.shape[0] // 2
    rows = 2 * half
    side = ka_ref.shape[0]

    @pl.when(pl.program_id(0) == 0)
    def _():
        me = place[0]
        row = lax.broadcasted_iota(jnp.int32, (half, rows), 0)
        col = lax.broadcasted_iota(jnp.int32, (half, rows), 1)
        lead = jnp.where(col < half, col, col - half) - row
        for query_half in range(2):
            query_span = span_order[2 * me + query_half]
            for piece, flip in enumerate(order):
                reach = []
                for key_half in range(2):
                    key_span = span_order[2 * (me ^ flip) + key_half]
                    granted = (block_mask[query_span, key_span] == 1) | (query_span == key_span)
                    reach.append(jnp.where(granted, (query_span - key_span) * half, -rows))
                limit = jnp.where(col < half, reach[0], reach[1])
                bias[query_half * half : (query_half + 1) * half, piece * rows : (piece + 1) * rows] = (
                    jnp.where(lead <= limit, 0.0, NEG_FILL)
                )

    contract = (((1,), (1,)), ((), ()))
    scale = HD ** (-0.5) * LOG2E
    for head in range(heads):
        cols = slice(head * HD, (head + 1) * HD)
        query = q_ref[:, cols]
        first = lax.dot_general(query, ka_ref[...], contract, preferred_element_type=F32)
        second = lax.dot_general(query, kb_ref[...], contract, preferred_element_type=F32)
        first = first * scale + bias[:, :side]
        second = second * scale + bias[:, side:]
        top = jnp.maximum(
            jnp.max(first, axis=1, keepdims=True), jnp.max(second, axis=1, keepdims=True)
        )
        first = jnp.exp2(first - top)
        second = jnp.exp2(second - top)
        total = jnp.sum(first, axis=1, keepdims=True) + jnp.sum(second, axis=1, keepdims=True)
        summed = jnp.dot(first.astype(BF16), va_ref[...], preferred_element_type=F32)
        summed = summed + jnp.dot(second.astype(BF16), vb_ref[...], preferred_element_type=F32)
        out_ref[:, cols] = (summed / total).astype(BF16)


def attention_call(place, span_order, block_mask, queries, near, far, order):
    rows, width = queries.shape
    local_kv = near.shape[1] // (2 * HD)
    heads = width // HD // local_kv
    side = near.shape[0]
    smem = pl.BlockSpec(memory_space=pltpu.SMEM)
    keys = pl.BlockSpec((side, HD), lambda g: (0, g))
    values = pl.BlockSpec((side, HD), lambda g: (0, local_kv + g))
    wide = pl.BlockSpec((rows, heads * HD), lambda g: (0, g))
    entries = rows * 2 * side * local_kv * heads
    return pl.pallas_call(
        functools.partial(attention_body, order=order, heads=heads),
        grid=(local_kv,),
        in_specs=[smem, smem, smem, wide, keys, keys, values, values],
        out_specs=wide,
        out_shape=jax.ShapeDtypeStruct((rows, width), BF16),
        scratch_shapes=[pltpu.VMEM((rows, 2 * side), F32)],
        cost_estimate=cost(entries * HD * 4, 4 * rows * width + 8 * side * local_kv * HD, entries),
        name="attention",
    )(place, span_order, block_mask, queries, near, far, near, far)


def front_body(x_ref, rim_ref, weight_ref, bias_ref, low_ref, bc_ref, act_ref, part_ref, low_sum, bc_sum):
    step = pl.program_id(0)
    rows = x_ref.shape[0]
    rank = low_ref.shape[1]
    extended = jnp.concatenate([rim_ref[...].astype(F32), x_ref[...].astype(F32)], axis=0)
    mixed = bias_ref[...]
    for tap in range(CONV):
        start = RIM - (CONV - 1) + tap
        mixed = mixed + weight_ref[tap : tap + 1, :] * extended[start : start + rows, :]
    act = (mixed / (1.0 + jnp.exp(-mixed))).astype(BF16)
    act_ref[...] = act
    low = jnp.dot(act, low_ref[...], preferred_element_type=F32)
    bc = jnp.dot(act, bc_ref[...], preferred_element_type=F32)

    @pl.when(step == 0)
    def _():
        low_sum[...] = low
        bc_sum[...] = bc

    @pl.when(step > 0)
    def _():
        low_sum[...] += low
        bc_sum[...] += bc

    @pl.when(step == pl.num_programs(0) - 1)
    def _():
        part_ref[:, :rank] = low_sum[...].astype(BF16)
        part_ref[:, rank:] = bc_sum[...].astype(BF16)


def front_call(mamba_in, rim, conv_weight, conv_bias, low_weight, bc_weight):
    rows, channels = mamba_in.shape
    rank, maps = low_weight.shape[1], bc_weight.shape[1]
    width = min(512, channels)
    block = pl.BlockSpec((rows, width), lambda i: (0, i))
    return pl.pallas_call(
        front_body,
        grid=(channels // width,),
        in_specs=[
            block,
            pl.BlockSpec((RIM, width), lambda i: (0, i)),
            pl.BlockSpec((CONV, width), lambda i: (0, i)),
            pl.BlockSpec((1, width), lambda i: (0, i)),
            pl.BlockSpec((width, rank), lambda i: (i, 0)),
            pl.BlockSpec((width, maps), lambda i: (i, 0)),
        ],
        out_specs=[block, pl.BlockSpec((rows, rank + maps), lambda i: (0, 0))],
        out_shape=[
            jax.ShapeDtypeStruct((rows, channels), BF16),
            jax.ShapeDtypeStruct((rows, rank + maps), BF16),
        ],
        scratch_shapes=[pltpu.VMEM((rows, rank), F32), pltpu.VMEM((rows, maps), F32)],
        cost_estimate=cost(
            2 * rows * channels * (rank + maps), channels * (4 * rows + 2 * (rank + maps)), rows * channels
        ),
        name="front",
    )(mamba_in, rim, conv_weight, conv_bias, low_weight, bc_weight)


def spread_rows(table, spread):
    rows = table.shape[0]
    tall = rows * STATE
    picker = lax.broadcasted_iota(jnp.int32, (tall, rows), 0) // STATE
    picker = picker == lax.broadcasted_iota(jnp.int32, (tall, rows), 1)
    picked = jnp.dot(
        picker.astype(F32).astype(BF16), table.astype(BF16), preferred_element_type=F32
    )
    state = lax.broadcasted_iota(jnp.int32, (tall, STATE), 0) % STATE
    kept = state == lax.broadcasted_iota(jnp.int32, (tall, STATE), 1)
    picked = jnp.where(kept, picked, 0.0).astype(BF16)
    spread[...] = jnp.dot(picked, jnp.ones((STATE, LANES), BF16), preferred_element_type=F32)


def advance(states, tiles, rates, step_ref, drive_ref, spread, base, offset):
    start = pl.multiple_of(base, TOKEN_BLOCK)
    inmap = spread[pl.ds(start * STATE + offset * STATE, STATE), :]
    moved = []
    for tile in range(tiles):
        lanes = pl.ds(tile * LANES, LANES)
        step = step_ref.at[pl.ds(start, TOKEN_BLOCK), lanes][pl.ds(offset, 1), :]
        drive = drive_ref.at[pl.ds(start, TOKEN_BLOCK), lanes][pl.ds(offset, 1), :]
        moved.append(jnp.exp2(step * rates[tile]) * states[tile] + drive * inmap)
    return moved


def softplus(v):
    small = jnp.exp(-jnp.abs(v))
    return jnp.maximum(v, 0.0) + jnp.log1p(small)


def ends_body(
    mine_ref, other_ref, gain_ref, weight_ref, bias_ref, rate_ref, act_ref, step_ref, end_ref, bc_ref, normed, spread, drive
):
    rows, width = act_ref.shape
    rank = gain_ref.shape[1]
    tiles = width // LANES

    @pl.when(pl.program_id(0) == 0)
    def _():
        low = mine_ref[:, :rank].astype(F32) + other_ref[:, :rank].astype(F32)
        scale = lax.rsqrt(jnp.mean(low * low, axis=1, keepdims=True) + 1e-06)
        normed[...] = (low * scale * gain_ref[...]).astype(BF16)
        bc = mine_ref[:, rank:].astype(F32) + other_ref[:, rank:].astype(F32)
        bc_ref[...] = bc
        spread_rows(bc[:, :STATE], spread)

    step = softplus(
        jnp.dot(normed[...], weight_ref[...], preferred_element_type=F32) + bias_ref[...]
    )
    step_ref[...] = step
    drive[...] = step * act_ref[...].astype(F32)
    end_ref[STATE:, :] = jnp.sum(step, axis=0, keepdims=True).astype(BF16)
    rates = [rate_ref[:, tile * LANES : (tile + 1) * LANES] for tile in range(tiles)]

    def block(index, states):
        states = list(states)
        for offset in range(TOKEN_BLOCK):
            states = advance(
                states, tiles, rates, step_ref, drive, spread, index * TOKEN_BLOCK, offset
            )
        return tuple(states)

    states = lax.fori_loop(
        0, rows // TOKEN_BLOCK, block, tuple(jnp.zeros((STATE, LANES), F32) for _ in range(tiles))
    )
    for tile in range(tiles):
        end_ref[:STATE, tile * LANES : (tile + 1) * LANES] = states[tile].astype(BF16)


def ends_call(mine, other, low_gain, dt_weight, dt_bias, rates, act):
    rows, channels = act.shape
    rank = dt_weight.shape[0]
    both = mine.shape[1]
    width = min(1024, channels)
    block = pl.BlockSpec((rows, width), lambda i: (0, i))
    whole = lambda shape: pl.BlockSpec(shape, lambda i: (0, 0))
    return pl.pallas_call(
        ends_body,
        grid=(channels // width,),
        in_specs=[
            whole((rows, both)),
            whole((rows, both)),
            whole((1, rank)),
            pl.BlockSpec((rank, width), lambda i: (0, i)),
            pl.BlockSpec((1, width), lambda i: (0, i)),
            pl.BlockSpec((STATE, width), lambda i: (0, i)),
            block,
        ],
        out_specs=[
            block,
            pl.BlockSpec((STATE + 1, width), lambda i: (0, i)),
            whole((rows, both - rank)),
        ],
        out_shape=[
            jax.ShapeDtypeStruct((rows, channels), F32),
            jax.ShapeDtypeStruct((STATE + 1, channels), BF16),
            jax.ShapeDtypeStruct((rows, both - rank), F32),
        ],
        scratch_shapes=[
            pltpu.VMEM((rows, rank), BF16),
            pltpu.VMEM((rows * STATE, LANES), F32),
            pltpu.VMEM((rows, width), F32),
        ],
        cost_estimate=cost(
            channels * rows * (2 * rank + 4 * STATE), channels * (6 * rows + 2 * rank), rows * channels * STATE
        ),
        name="ends",
    )(mine, other, low_gain, dt_weight, dt_bias, rates, act)


def scan_body(
    step_ref, act_ref, gate_ref, bc_ref, rate_ref, enter_ref, skip_ref, out_ref, spread, outmap, drive, even, odd
):
    rows, width = act_ref.shape
    tiles = width // LANES
    deep = TOKEN_BLOCK * STATE

    @pl.when(pl.program_id(0) == 0)
    def _():
        spread_rows(bc_ref[:, :STATE], spread)
        place = lax.broadcasted_iota(jnp.int32, (STATE, deep), 1)
        repeat = (place % STATE) == lax.broadcasted_iota(jnp.int32, (STATE, deep), 0)
        wide = jnp.dot(
            bc_ref[:, STATE:].astype(BF16), repeat.astype(F32).astype(BF16), preferred_element_type=F32
        )
        token = lax.broadcasted_iota(jnp.int32, (rows, deep), 0) % TOKEN_BLOCK
        own = token == lax.broadcasted_iota(jnp.int32, (rows, deep), 1) // STATE
        outmap[...] = jnp.where(own, wide, 0.0).astype(BF16)

    drive[...] = step_ref[...] * act_ref[...].astype(F32)
    rates = [rate_ref[:, tile * LANES : (tile + 1) * LANES] for tile in range(tiles)]

    def walk(index, states, held):
        states = list(states)
        for offset in range(TOKEN_BLOCK):
            states = advance(
                states, tiles, rates, step_ref, drive, spread, index * TOKEN_BLOCK, offset
            )
            for tile in range(tiles):
                held[offset * STATE : (offset + 1) * STATE, tile * LANES : (tile + 1) * LANES] = states[tile]
        return tuple(states)

    def emit(index, held):
        span = pl.ds(pl.multiple_of(index * TOKEN_BLOCK, TOKEN_BLOCK), TOKEN_BLOCK)
        summed = jnp.dot(outmap[span, :], held[...].astype(BF16), preferred_element_type=F32)
        summed = summed + skip_ref[...] * act_ref[span, :].astype(F32)
        gate = gate_ref[span, :].astype(F32)
        out_ref[span, :] = (summed * (gate / (1.0 + jnp.exp(-gate)))).astype(BF16)

    def pair(index, states):
        states = walk(2 * index + 1, states, odd)
        emit(2 * index, even)
        states = walk(2 * index + 2, states, even)
        emit(2 * index + 1, odd)
        return states

    blocks = rows // TOKEN_BLOCK
    states = tuple(enter_ref[:, tile * LANES : (tile + 1) * LANES] for tile in range(tiles))
    states = walk(0, states, even)
    states = lax.fori_loop(0, blocks // 2 - 1, pair, states)
    walk(blocks - 1, states, odd)
    emit(blocks - 2, even)
    emit(blocks - 1, odd)


def scan_call(step, act, gate, bc, rates, enter, skip):
    rows, channels = act.shape
    width = min(1024, channels)
    block = pl.BlockSpec((rows, width), lambda i: (0, i))
    table = pl.BlockSpec((STATE, width), lambda i: (0, i))
    deep = TOKEN_BLOCK * STATE
    return pl.pallas_call(
        scan_body,
        grid=(channels // width,),
        in_specs=[
            block,
            block,
            block,
            pl.BlockSpec(bc.shape, lambda i: (0, 0)),
            table,
            table,
            pl.BlockSpec((1, width), lambda i: (0, i)),
        ],
        out_specs=block,
        out_shape=jax.ShapeDtypeStruct((rows, channels), BF16),
        scratch_shapes=[
            pltpu.VMEM((rows * STATE, LANES), F32),
            pltpu.VMEM((rows, deep), BF16),
            pltpu.VMEM((rows, width), F32),
            pltpu.VMEM((deep, width), F32),
            pltpu.VMEM((deep, width), F32),
        ],
        cost_estimate=cost(8 * channels * rows * STATE, channels * rows * 10, rows * channels * STATE),
        name="scan",
    )(step, act, gate, bc, rates, enter, skip)


def entering(ends, rates):
    place = lax.axis_index("ctx")
    count = lax.axis_size("ctx")
    total = (ends[STATE:].astype(F32), ends[:STATE].astype(F32))
    before = tuple(jnp.zeros_like(part) for part in total)

    def join(early, late):
        return (early[0] + late[0], early[1] * jnp.exp2(rates * late[0]) + late[1])

    packed = ends
    for step in bits_of(count):
        last = 2 * step == count
        if last:
            got = lax.ppermute(packed, "ctx", [(i, i ^ step) for i in range(count) if not i & step])
        else:
            got = swap(packed, "ctx", step)
        got = (got[STATE:].astype(F32), got[:STATE].astype(F32))
        upper = (place & step) != 0
        joined = join(got, before)
        before = tuple(jnp.where(upper, new, old) for new, old in zip(joined, before))
        if not last:
            above, below = join(got, total), join(total, got)
            total = tuple(jnp.where(upper, a, b) for a, b in zip(above, below))
            packed = jnp.concatenate([total[1], total[0]], axis=0).astype(BF16)
    return before[1]


def per_device(
    queries,
    key_heads,
    value_heads,
    span_order,
    block_mask,
    mamba_in,
    gate_in,
    conv_weight,
    conv_bias,
    low_weight,
    bc_weight,
    low_gain,
    dt_weight,
    dt_bias,
    rate_log,
    skip_gain,
):
    row_count = queries.shape[0]
    count = lax.axis_size("ctx")
    head_devices = lax.axis_size("head")
    place = lax.axis_index("ctx")

    rim = lax.ppermute(mamba_in[row_count - RIM :], "ctx", [(i, i + 1) for i in range(count - 1)])

    kv_count = key_heads.shape[1] // HD
    local_kv = max(1, kv_count // head_devices)
    query_local = queries.shape[1] // HD
    group_size = query_local * head_devices // kv_count
    kv_start = lax.axis_index("head") * query_local // group_size
    near = jnp.concatenate(
        [
            lax.dynamic_slice_in_dim(key_heads, kv_start * HD, local_kv * HD, 1),
            lax.dynamic_slice_in_dim(value_heads, kv_start * HD, local_kv * HD, 1),
        ],
        axis=1,
    )
    order = [0]
    steps = bits_of(count)[::-1]
    for step in steps:
        far = swap(near, "ctx", step)
        order = order + [flip ^ step for flip in order]
        if step != steps[-1]:
            near = jnp.concatenate([near, far], axis=0)

    rates = (jnp.exp(rate_log) * -LOG2E).T
    act, part = front_call(
        mamba_in, rim, conv_weight, conv_bias[None, :], low_weight, bc_weight
    )
    steps = bits_of(head_devices)
    for step in steps:
        other = swap(part, "head", step)
        if step != steps[-1]:
            part = (part.astype(F32) + other.astype(F32)).astype(BF16)
    step_dt, ends, bc = ends_call(
        part, other, low_gain[None, :], dt_weight, dt_bias[None, :], rates, act
    )
    enter = entering(ends, rates)
    attn_out = attention_call(
        place.astype(jnp.int32)[None], span_order, block_mask, queries, near, far, tuple(order)
    )
    mamba_out = scan_call(step_dt, act, gate_in, bc, rates, enter, skip_gain[None, :])
    return (attn_out, mamba_out)


def solution(mesh):
    in_specs = (
        P("ctx", "head"),
        P("ctx", None),
        P("ctx", None),
        P(),
        P(),
        P("ctx", "head"),
        P("ctx", "head"),
        P(None, "head"),
        P("head"),
        P("head", None),
        P("head", None),
        P(),
        P(None, "head"),
        P("head"),
        P("head", None),
        P("head"),
    )
    out_specs = (P("ctx", "head"), P("ctx", "head"))
    return jax.shard_map(
        per_device, mesh=mesh, in_specs=in_specs, out_specs=out_specs, check_vma=False
    )
```

```python
import functools

import jax
import jax.numpy as jnp
from jax import lax
from jax.experimental import pallas as pl
from jax.experimental.pallas import tpu as pltpu
from jax.sharding import PartitionSpec as P


HD = 128
STATE = 16
CONV = 4
RIM = 8
LANES = 128
TOKEN_BLOCK = 16
LOG2E = 1.4426950408889634
NEG_FILL = -1e30
F32 = jnp.float32
BF16 = jnp.bfloat16
CONTRACT_LAST = (((1,), (1,)), ((), ()))
WIDE = 40
FRONT_WIDTH = 1024
FRONT_GRANT = 55
END_BLOCK = 32


def swap(value, axis, step):
    count = lax.axis_size(axis)
    return lax.ppermute(value, axis, [(i, i ^ step) for i in range(count)])


def bits_of(count):
    steps = []
    while 2 ** len(steps) < count:
        steps.append(2 ** len(steps))
    return steps


def after(values):
    return lax.optimization_barrier(values)


def grant(mib):
    return pltpu.CompilerParams(vmem_limit_bytes=mib * 2**20)


def resident():
    return pl.BlockSpec(memory_space=pltpu.VMEM)


def cost(flops, moved, exps=0):
    return pl.CostEstimate(flops=flops, bytes_accessed=moved, transcendentals=exps)


def attention_body(
    place, span_order, block_mask, q_ref, near_ref, far_ref, *refs, order, heads, kv_head
):
    out_ref, bias = refs[-2:]
    kv_width = near_ref.shape[1] // 2
    key_lanes = pl.ds(kv_head * HD, HD)
    value_lanes = pl.ds(kv_width + kv_head * HD, HD)
    ka_ref, kb_ref = near_ref.at[:, key_lanes], far_ref.at[:, key_lanes]
    va_ref, vb_ref = near_ref.at[:, value_lanes], far_ref.at[:, value_lanes]
    half = q_ref.shape[0] // 2
    rows = 2 * half
    side = ka_ref.shape[0]

    def fill():
        me = place[0]
        row = lax.broadcasted_iota(jnp.int32, (half, rows), 0)
        col = lax.broadcasted_iota(jnp.int32, (half, rows), 1)
        lead = jnp.where(col < half, col, col - half) - row
        for query_half in range(2):
            query_span = span_order[2 * me + query_half]
            for piece, flip in enumerate(order):
                reach = []
                for key_half in range(2):
                    key_span = span_order[2 * (me ^ flip) + key_half]
                    granted = (block_mask[query_span, key_span] == 1) | (query_span == key_span)
                    reach.append(jnp.where(granted, (query_span - key_span) * half, -rows))
                limit = jnp.where(col < half, reach[0], reach[1])
                bias[query_half * half : (query_half + 1) * half, piece * rows : (piece + 1) * rows] = (
                    jnp.where(lead <= limit, 0.0, NEG_FILL)
                )

    fill()

    scale = HD ** (-0.5) * LOG2E
    for head in range(heads):
        cols = slice(head * HD, (head + 1) * HD)
        query = q_ref[:, cols]
        first = lax.dot_general(query, ka_ref[...], CONTRACT_LAST, preferred_element_type=F32)
        second = lax.dot_general(query, kb_ref[...], CONTRACT_LAST, preferred_element_type=F32)
        first = first * scale + bias[:, :side]
        second = second * scale + bias[:, side:]
        top = jnp.maximum(
            jnp.max(first, axis=1, keepdims=True), jnp.max(second, axis=1, keepdims=True)
        )
        first = jnp.exp2(first - top)
        second = jnp.exp2(second - top)
        total = jnp.sum(first, axis=1, keepdims=True) + jnp.sum(second, axis=1, keepdims=True)
        summed = jnp.dot(first.astype(BF16), va_ref[...], preferred_element_type=F32)
        summed = summed + jnp.dot(second.astype(BF16), vb_ref[...], preferred_element_type=F32)
        out_ref[:, cols] = (summed / total).astype(BF16)


def attention_call(place, span_order, block_mask, queries, near, far, so_far, turn, turns, order):
    rows, width = queries.shape
    local_kv = near.shape[1] // (2 * HD)
    heads = width // HD // turns
    kv_head = turn * local_kv // turns
    side = near.shape[0]
    smem = pl.BlockSpec(memory_space=pltpu.SMEM)
    wide = pl.BlockSpec((rows, heads * HD), lambda i: (0, turn))
    entries = rows * 2 * side * heads
    operands = [place, span_order, block_mask, queries, near, far]
    specs = [smem, smem, smem, wide, resident(), resident()]
    aliases = {}
    if so_far is not None:
        aliases = {len(operands): 0}
        operands.append(so_far)
        specs.append(pl.BlockSpec(memory_space=pl.ANY))
    return pl.pallas_call(
        functools.partial(attention_body, order=order, heads=heads, kv_head=kv_head),
        grid=(1,),
        in_specs=specs,
        out_specs=wide,
        out_shape=jax.ShapeDtypeStruct((rows, width), BF16),
        scratch_shapes=[pltpu.VMEM((rows, 2 * side), F32)],
        input_output_aliases=aliases,
        cost_estimate=cost(entries * HD * 4, 4 * rows * heads * HD + 8 * side * HD, entries),
        compiler_params=grant(WIDE),
        name="attention",
    )(*operands)


def fold_rows(table, width):
    rows, narrow = table.shape
    short = rows * narrow // width
    return jnp.concatenate([table[at : at + short] for at in range(0, rows, short)], axis=1)


def unfold_rows(folded, narrow):
    return jnp.concatenate(
        [folded[:, at : at + narrow] for at in range(0, folded.shape[1], narrow)], axis=0
    )


def front_body(*refs):
    sources, (rim_ref, act_ref, part_ref), refs = refs[:5], refs[5:8], refs[8:]
    targets, (low_sum, bc_sum, sems) = refs[:5], refs[5:]
    x_ref, weight_ref, bias_ref, low_ref, bc_ref = targets
    step = pl.program_id(0)
    width = act_ref.shape[1]
    rows = x_ref.shape[0]
    rank = low_ref.shape[1]
    here = pl.ds(pl.multiple_of(step * width, LANES), width)

    def fetches(turn):
        span = pl.ds(pl.multiple_of(turn * width, LANES), width)
        copies = []
        for index, (source, target) in enumerate(zip(sources, targets)):
            at = (span,) if target is low_ref else (slice(None), span)
            copies.append(pltpu.make_async_copy(source.at[at], target.at[at], sems.at[index, turn]))
        return copies

    @pl.when(step == 0)
    def _():
        for turn in range(sems.shape[1]):
            for copy in fetches(turn):
                copy.start()

    for copy in fetches(step):
        copy.wait()

    extended = jnp.concatenate([rim_ref[:, here].astype(F32), x_ref[:, here].astype(F32)], axis=0)
    mixed = bias_ref[:, here]
    for tap in range(CONV):
        start = RIM - (CONV - 1) + tap
        mixed = mixed + weight_ref[tap : tap + 1, here] * extended[start : start + rows, :]
    act = (mixed / (1.0 + jnp.exp(-mixed))).astype(BF16)
    act_ref[...] = act
    low = jnp.dot(act, low_ref[here, :], preferred_element_type=F32)
    bc = lax.dot_general(act, bc_ref[:, here], CONTRACT_LAST, preferred_element_type=F32)

    @pl.when(step == 0)
    def _():
        low_sum[...] = low
        bc_sum[...] = bc

    @pl.when(step > 0)
    def _():
        low_sum[...] += low
        bc_sum[...] += bc

    @pl.when(step == pl.num_programs(0) - 1)
    def _():
        part_ref[:rows, :] = low_sum[...].astype(BF16)
        part_ref[rows:, :] = fold_rows(bc_sum[...], rank).astype(BF16)


def front_call(mamba_in, rim, conv_weight, conv_bias, low_weight, bc_weight):
    rows, channels = mamba_in.shape
    rank, maps = low_weight.shape[1], bc_weight.shape[0]
    tall = rows + rows * maps // rank
    width = min(FRONT_WIDTH, channels)
    fetched = [mamba_in, conv_weight, conv_bias, low_weight, bc_weight]
    return pl.pallas_call(
        front_body,
        grid=(channels // width,),
        in_specs=[pl.BlockSpec(memory_space=pl.ANY)] * len(fetched) + [resident()],
        out_specs=[pl.BlockSpec((rows, width), lambda i: (0, i)), resident()],
        out_shape=[
            jax.ShapeDtypeStruct((rows, channels), BF16),
            jax.ShapeDtypeStruct((tall, rank), BF16),
        ],
        scratch_shapes=[
            *[pltpu.VMEM(array.shape, array.dtype) for array in fetched],
            pltpu.VMEM((rows, rank), F32),
            pltpu.VMEM((rows, maps), F32),
            pltpu.SemaphoreType.DMA((len(fetched), channels // width)),
        ],
        cost_estimate=cost(
            2 * rows * channels * (rank + maps), channels * (4 * rows + 2 * (rank + maps)), rows * channels
        ),
        compiler_params=grant(FRONT_GRANT),
        name="front",
    )(*fetched, rim)


def spread_rows(table, spread):
    rows = table.shape[0]
    tall = rows * STATE
    picker = lax.broadcasted_iota(jnp.int32, (tall, rows), 0) // STATE
    picker = picker == lax.broadcasted_iota(jnp.int32, (tall, rows), 1)
    picked = jnp.dot(picker.astype(F32).astype(BF16), table.astype(BF16), preferred_element_type=F32)
    state = lax.broadcasted_iota(jnp.int32, (tall, STATE), 0) % STATE
    kept = state == lax.broadcasted_iota(jnp.int32, (tall, STATE), 1)
    picked = jnp.where(kept, picked, 0.0).astype(BF16)
    spread[...] = jnp.dot(picked, jnp.ones((STATE, LANES), BF16), preferred_element_type=F32)


def tail_width(channels):
    return max(LANES, channels // STATE)


def sums_of(packed, channels):
    wide = tail_width(channels)
    return jnp.concatenate(
        [packed[row : row + 1, channels : channels + wide] for row in range(channels // wide)], axis=1
    )


def store_sums(ref, row, channels):
    wide = tail_width(channels)
    pieces = [row[:, at : at + wide] for at in range(0, channels, wide)]
    spare = STATE - len(pieces)
    if spare:
        pieces.append(jnp.zeros((spare, wide), F32))
    ref[:, channels:] = jnp.concatenate(pieces, axis=0).astype(BF16)


def advance(states, tiles, rates, step_ref, drive_ref, spread, base, offset, size):
    start = pl.multiple_of(base, size)
    inmap = spread[pl.ds(start * STATE + offset * STATE, STATE), :]
    moved = []
    for tile in range(tiles):
        lanes = pl.ds(tile * LANES, LANES)
        step = step_ref.at[pl.ds(start, size), lanes][pl.ds(offset, 1), :]
        drive = drive_ref.at[pl.ds(start, size), lanes][pl.ds(offset, 1), :]
        moved.append(jnp.exp2(step * rates[:, lanes]) * states[tile] + drive * inmap)
    return moved


def softplus(v):
    return jnp.maximum(v, 0.0) + jnp.log1p(jnp.exp(-jnp.abs(v)))


def rates_of(log_ref):
    return jnp.exp(log_ref[...]) * -LOG2E


def split_lanes(value):
    return [value[:, start : start + LANES] for start in range(0, value.shape[1], LANES)]


def ends_body(
    mine_ref, other_ref, gain_ref, weight_ref, bias_ref, log_ref, act_ref, step_ref, end_ref, bc_ref, normed, spread, drive, sums, rates, wide_step
):
    rows, width = act_ref.shape
    maps = bc_ref.shape[1]
    channels = sums.shape[1]
    tiles = width // LANES
    here = pl.multiple_of(pl.program_id(0) * width, LANES)

    @pl.when(pl.program_id(0) == 0)
    def _():
        both = mine_ref[...].astype(F32) + other_ref[...].astype(F32)
        low = both[:rows]
        scale = lax.rsqrt(jnp.mean(low * low, axis=1, keepdims=True) + 1e-06)
        normed[...] = (low * scale * gain_ref[...]).astype(BF16)
        bc = unfold_rows(both[rows:], maps)
        bc_ref[...] = bc
        spread_rows(bc[:, :STATE], spread)

    step = softplus(
        jnp.dot(normed[...], weight_ref[...], preferred_element_type=F32) + bias_ref[...]
    )
    wide_step[...] = step
    step_ref[...] = step.astype(BF16)
    drive[...] = step * act_ref[...].astype(F32)
    sums[:, pl.ds(here, width)] = jnp.sum(step, axis=0, keepdims=True)
    rates[...] = rates_of(log_ref)

    def block(index, states):
        states = list(states)
        for offset in range(END_BLOCK):
            states = advance(
                states, tiles, rates, wide_step, drive, spread, index * END_BLOCK, offset, END_BLOCK
            )
        return tuple(states)

    states = lax.fori_loop(
        0, rows // END_BLOCK, block, tuple(jnp.zeros((STATE, LANES), F32) for _ in range(tiles))
    )
    for tile in range(tiles):
        lanes = pl.ds(pl.multiple_of(here + tile * LANES, LANES), LANES)
        end_ref[:, lanes] = states[tile].astype(BF16)

    @pl.when(pl.program_id(0) == pl.num_programs(0) - 1)
    def _():
        store_sums(end_ref, sums[...], channels)


def ends_call(mine, other, low_gain, dt_weight, dt_bias, rate_log, act):
    rows, channels = act.shape
    tall, rank = mine.shape
    maps = (tall - rows) * rank // rows
    width = min(1024, channels)
    block = lambda height: pl.BlockSpec((height, width), lambda i: (0, i))
    whole = lambda shape: pl.BlockSpec(shape, lambda i: (0, 0))
    packed = (STATE, channels + tail_width(channels))
    return pl.pallas_call(
        ends_body,
        grid=(channels // width,),
        in_specs=[
            resident(),
            resident(),
            whole((1, rank)),
            block(rank),
            block(1),
            block(STATE),
            block(rows),
        ],
        out_specs=[block(rows), resident(), whole((rows, maps))],
        out_shape=[
            jax.ShapeDtypeStruct((rows, channels), BF16),
            jax.ShapeDtypeStruct(packed, BF16),
            jax.ShapeDtypeStruct((rows, maps), F32),
        ],
        scratch_shapes=[
            pltpu.VMEM((rows, rank), BF16),
            pltpu.VMEM((rows * STATE, LANES), F32),
            pltpu.VMEM((rows, width), F32),
            pltpu.VMEM((1, channels), F32),
            pltpu.VMEM((STATE, width), F32),
            pltpu.VMEM((rows, width), F32),
        ],
        cost_estimate=cost(
            channels * rows * (2 * rank + 4 * STATE), channels * (6 * rows + 2 * rank), rows * channels * STATE
        ),
        compiler_params=grant(WIDE),
        name="ends",
    )(mine, other, low_gain, dt_weight, dt_bias, rate_log, act)


def join_body(place, own_ref, got_ref, log_ref, out_ref, *, step):
    channels = log_ref.shape[1]
    upper = (place[0] & step) != 0
    own = own_ref[...].astype(F32)
    got = got_ref[...].astype(F32)
    early = jnp.where(upper, got, own)
    late = jnp.where(upper, own, got)
    decay = jnp.exp2(rates_of(log_ref) * sums_of(late, channels))
    out_ref[:, :channels] = (early[:, :channels] * decay + late[:, :channels]).astype(BF16)
    out_ref[:, channels:] = (early[:, channels:] + late[:, channels:]).astype(BF16)


def join_call(place, own, got, rate_log, step):
    return pl.pallas_call(
        functools.partial(join_body, step=step),
        in_specs=[pl.BlockSpec(memory_space=pltpu.SMEM), resident(), resident(), resident()],
        out_specs=resident(),
        out_shape=jax.ShapeDtypeStruct(own.shape, BF16),
        cost_estimate=cost(8 * own.size, 10 * own.size, own.size),
        compiler_params=grant(16),
        name="join",
    )(place, own, got, rate_log)


def scan_body(place, *refs, steps):
    got_refs, refs = refs[: len(steps)], refs[len(steps) :]
    step_ref, act_ref, gate_ref, bc_ref, log_ref, skip_ref, out_ref = refs[:7]
    spread, outmap, drive, enter, rates, wide_step, even, odd = refs[7:]
    rows, width = act_ref.shape
    tiles = width // LANES
    channels = enter.shape[1]
    deep = TOKEN_BLOCK * STATE
    here = pl.multiple_of(pl.program_id(0) * width, LANES)

    @pl.when(pl.program_id(0) == 0)
    def _():
        every = rates_of(log_ref)
        state = jnp.zeros((STATE, channels), F32)
        passed = jnp.zeros((1, channels), F32)
        for step, got_ref in zip(steps, got_refs):
            upper = (place[0] & step) != 0
            got = got_ref[...].astype(F32)
            state = jnp.where(upper, got[:, :channels] * jnp.exp2(every * passed) + state, state)
            passed = jnp.where(upper, sums_of(got, channels) + passed, passed)
        enter[...] = state

        spread_rows(bc_ref[:, :STATE], spread)
        place_in = lax.broadcasted_iota(jnp.int32, (STATE, deep), 1)
        repeat = (place_in % STATE) == lax.broadcasted_iota(jnp.int32, (STATE, deep), 0)
        wide = jnp.dot(
            bc_ref[:, STATE:].astype(BF16), repeat.astype(F32).astype(BF16), preferred_element_type=F32
        )
        token = lax.broadcasted_iota(jnp.int32, (rows, deep), 0) % TOKEN_BLOCK
        own = token == lax.broadcasted_iota(jnp.int32, (rows, deep), 1) // STATE
        outmap[...] = jnp.where(own, wide, 0.0).astype(BF16)

    wide_step[...] = step_ref[...].astype(F32)
    drive[...] = wide_step[...] * act_ref[...].astype(F32)
    rates[...] = jnp.exp(log_ref[:, pl.ds(here, width)]) * -LOG2E

    def walk(index, states, held):
        states = list(states)
        for offset in range(TOKEN_BLOCK):
            states = advance(
                states, tiles, rates, wide_step, drive, spread, index * TOKEN_BLOCK, offset, TOKEN_BLOCK
            )
            for tile in range(tiles):
                held[offset * STATE : (offset + 1) * STATE, tile * LANES : (tile + 1) * LANES] = states[tile]
        return tuple(states)

    def emit(index, held):
        span = pl.ds(pl.multiple_of(index * TOKEN_BLOCK, TOKEN_BLOCK), TOKEN_BLOCK)
        summed = jnp.dot(outmap[span, :], held[...].astype(BF16), preferred_element_type=F32)
        summed = summed + skip_ref[...] * act_ref[span, :].astype(F32)
        gate = gate_ref[span, :].astype(F32)
        out_ref[span, :] = (summed * (gate / (1.0 + jnp.exp(-gate)))).astype(BF16)

    def pair(index, states):
        states = walk(2 * index + 1, states, odd)
        emit(2 * index, even)
        states = walk(2 * index + 2, states, even)
        emit(2 * index + 1, odd)
        return states

    blocks = rows // TOKEN_BLOCK
    states = walk(0, split_lanes(enter[:, pl.ds(here, width)]), even)
    states = lax.fori_loop(0, blocks // 2 - 1, pair, states)
    walk(blocks - 1, states, odd)
    emit(blocks - 2, even)
    emit(blocks - 1, odd)


def scan_call(place, gots, step, act, gate, bc, rate_log, skip):
    rows, channels = act.shape
    width = min(1024, channels)
    block = lambda height: pl.BlockSpec((height, width), lambda i: (0, i))
    whole = lambda shape: pl.BlockSpec(shape, lambda i: (0, 0))
    deep = TOKEN_BLOCK * STATE
    return pl.pallas_call(
        functools.partial(scan_body, steps=bits_of(2 ** len(gots))),
        grid=(channels // width,),
        in_specs=[
            pl.BlockSpec(memory_space=pltpu.SMEM),
            *[resident() for got in gots],
            block(rows),
            block(rows),
            block(rows),
            whole(bc.shape),
            whole(rate_log.shape),
            block(1),
        ],
        out_specs=block(rows),
        out_shape=jax.ShapeDtypeStruct((rows, channels), BF16),
        scratch_shapes=[
            pltpu.VMEM((rows * STATE, LANES), F32),
            pltpu.VMEM((rows, deep), BF16),
            pltpu.VMEM((rows, width), F32),
            pltpu.VMEM((STATE, channels), F32),
            pltpu.VMEM((STATE, width), F32),
            pltpu.VMEM((rows, width), F32),
            pltpu.VMEM((deep, width), F32),
            pltpu.VMEM((deep, width), F32),
        ],
        cost_estimate=cost(8 * channels * rows * STATE, channels * rows * 10, rows * channels * STATE),
        compiler_params=grant(WIDE),
        name="scan",
    )(place, *gots, step, act, gate, bc, rate_log, skip)


def per_device(
    queries,
    key_heads,
    value_heads,
    span_order,
    block_mask,
    mamba_in,
    gate_in,
    conv_weight,
    conv_bias,
    low_weight,
    bc_weight,
    low_gain,
    dt_weight,
    dt_bias,
    rate_log,
    skip_gain,
):
    row_count = queries.shape[0]
    count = lax.axis_size("ctx")
    head_devices = lax.axis_size("head")
    place = lax.axis_index("ctx").astype(jnp.int32)[None]

    tail, key_heads, value_heads = after((mamba_in[row_count - RIM :], key_heads, value_heads))
    rim = lax.ppermute(tail, "ctx", [(i, i + 1) for i in range(count - 1)])

    kv_count = key_heads.shape[1] // HD
    local_kv = max(1, kv_count // head_devices)
    query_local = queries.shape[1] // HD
    group_size = query_local * head_devices // kv_count
    kv_start = lax.axis_index("head") * query_local // group_size
    near = jnp.concatenate(
        [
            lax.dynamic_slice_in_dim(key_heads, kv_start * HD, local_kv * HD, 1),
            lax.dynamic_slice_in_dim(value_heads, kv_start * HD, local_kv * HD, 1),
        ],
        axis=1,
    )
    kv_hops = bits_of(count)[::-1]
    kv_hops[:2] = kv_hops[:2][::-1]
    order = [0]
    for hop in kv_hops:
        order = order + [flip ^ hop for flip in order]
    far = swap(near, "ctx", kv_hops[0])

    def gather_on(near, far, turn):
        near = jnp.concatenate([near, far], axis=0)
        return near, swap(near, "ctx", kv_hops[turn])

    logs = rate_log.T
    if len(kv_hops) > 1:
        near, far = gather_on(near, far, 1)
        rim, near = after((rim, near))
    act, part = front_call(mamba_in, rim, conv_weight, conv_bias[None, :], low_weight, bc_weight.T)
    hops = bits_of(head_devices)
    for hop in hops:
        other = swap(part, "head", hop)
        if hop != hops[-1]:
            part = (part.astype(F32) + other.astype(F32)).astype(BF16)
    for turn in range(2, len(kv_hops)):
        near, far = gather_on(near, far, turn)
    step_dt, packed, bc = ends_call(
        part, other, low_gain[None, :], dt_weight, dt_bias[None, :], logs, act
    )

    attn_out = None
    gots = []
    hops = bits_of(count)
    runs = local_kv * (2 if query_local // local_kv % 2 == 0 else 1)
    for turn, hop in enumerate(hops):
        if 2 * hop == count:
            pairs = [(i, i ^ hop) for i in range(count) if not i & hop]
            got = lax.ppermute(packed, "ctx", pairs)
        else:
            got = swap(packed, "ctx", hop)
        taken = [turn] if turn + 1 < len(hops) else range(turn, runs)
        for run in taken:
            if run >= runs:
                continue
            packed, queries, near, attn_out = after((packed, queries, near, attn_out))
            attn_out = attention_call(
                place, span_order, block_mask, queries, near, far, attn_out, run, runs, tuple(order)
            )
        got, attn_out = after((got, attn_out))
        if 2 * hop < count:
            packed = join_call(place, packed, got, logs, hop)
        gots.append(got)
    mamba_out = scan_call(place, gots, step_dt, act, gate_in, bc, logs, skip_gain[None, :])
    return (attn_out, mamba_out)


def solution(mesh):
    in_specs = (
        P("ctx", "head"),
        P("ctx", None),
        P("ctx", None),
        P(),
        P(),
        P("ctx", "head"),
        P("ctx", "head"),
        P(None, "head"),
        P("head"),
        P("head", None),
        P("head", None),
        P(),
        P(None, "head"),
        P("head"),
        P("head", None),
        P("head"),
    )
    out_specs = (P("ctx", "head"), P("ctx", "head"))

    return jax.shard_map(
        per_device, mesh=mesh, in_specs=in_specs, out_specs=out_specs, check_vma=False
    )
```

```python
import functools

import jax
import jax.numpy as jnp
from jax import lax
from jax.experimental import pallas as pl
from jax.experimental.pallas import tpu as pltpu
from jax.sharding import PartitionSpec as P


HD = 128
STATE = 16
CONV = 4
RIM = 8
LANES = 128
TOKEN_BLOCK = 16
LOG2E = 1.4426950408889634
NEG_FILL = -1e30
F32 = jnp.float32
BF16 = jnp.bfloat16
CONTRACT_LAST = (((1,), (1,)), ((), ()))
WIDE = 40
FRONT_WIDTH = 1024
FRONT_GRANT = 55
END_BLOCK = 32


def swap(value, axis, step):
    count = lax.axis_size(axis)
    return lax.ppermute(value, axis, [(i, i ^ step) for i in range(count)])


def bits_of(count):
    steps = []
    while 2 ** len(steps) < count:
        steps.append(2 ** len(steps))
    return steps


def after(values):
    return lax.optimization_barrier(values)


def grant(mib):
    return pltpu.CompilerParams(vmem_limit_bytes=mib * 2**20)


def resident():
    return pl.BlockSpec(memory_space=pltpu.VMEM)


def cost(flops, moved, exps=0):
    return pl.CostEstimate(flops=flops, bytes_accessed=moved, transcendentals=exps)


def attention_body(
    place, span_order, block_mask, q_ref, near_ref, far_ref, *refs, order, heads, kv_head
):
    out_ref, bias = refs[-2:]
    kv_width = near_ref.shape[1] // 2
    key_lanes = pl.ds(kv_head * HD, HD)
    value_lanes = pl.ds(kv_width + kv_head * HD, HD)
    ka_ref, kb_ref = near_ref.at[:, key_lanes], far_ref.at[:, key_lanes]
    va_ref, vb_ref = near_ref.at[:, value_lanes], far_ref.at[:, value_lanes]
    half = q_ref.shape[0] // 2
    rows = 2 * half
    side = ka_ref.shape[0]

    def fill():
        me = place[0]
        row = lax.broadcasted_iota(jnp.int32, (half, rows), 0)
        col = lax.broadcasted_iota(jnp.int32, (half, rows), 1)
        lead = jnp.where(col < half, col, col - half) - row
        for query_half in range(2):
            query_span = span_order[2 * me + query_half]
            for piece, flip in enumerate(order):
                reach = []
                for key_half in range(2):
                    key_span = span_order[2 * (me ^ flip) + key_half]
                    granted = (block_mask[query_span, key_span] == 1) | (query_span == key_span)
                    reach.append(jnp.where(granted, (query_span - key_span) * half, -rows))
                limit = jnp.where(col < half, reach[0], reach[1])
                bias[query_half * half : (query_half + 1) * half, piece * rows : (piece + 1) * rows] = (
                    jnp.where(lead <= limit, 0.0, NEG_FILL)
                )

    fill()

    scale = HD ** (-0.5) * LOG2E
    for head in range(heads):
        cols = slice(head * HD, (head + 1) * HD)
        query = q_ref[:, cols]
        first = lax.dot_general(query, ka_ref[...], CONTRACT_LAST, preferred_element_type=F32)
        second = lax.dot_general(query, kb_ref[...], CONTRACT_LAST, preferred_element_type=F32)
        first = first * scale + bias[:, :side]
        second = second * scale + bias[:, side:]
        top = jnp.maximum(
            jnp.max(first, axis=1, keepdims=True), jnp.max(second, axis=1, keepdims=True)
        )
        first = jnp.exp2(first - top)
        second = jnp.exp2(second - top)
        total = jnp.sum(first, axis=1, keepdims=True) + jnp.sum(second, axis=1, keepdims=True)
        summed = jnp.dot(first.astype(BF16), va_ref[...], preferred_element_type=F32)
        summed = summed + jnp.dot(second.astype(BF16), vb_ref[...], preferred_element_type=F32)
        out_ref[:, cols] = (summed / total).astype(BF16)


def attention_call(place, span_order, block_mask, queries, near, far, so_far, turn, turns, order):
    rows, width = queries.shape
    local_kv = near.shape[1] // (2 * HD)
    heads = width // HD // turns
    kv_head = turn * local_kv // turns
    side = near.shape[0]
    smem = pl.BlockSpec(memory_space=pltpu.SMEM)
    wide = pl.BlockSpec((rows, heads * HD), lambda i: (0, turn))
    entries = rows * 2 * side * heads
    operands = [place, span_order, block_mask, queries, near, far]
    specs = [smem, smem, smem, wide, resident(), resident()]
    aliases = {}
    if so_far is not None:
        aliases = {len(operands): 0}
        operands.append(so_far)
        specs.append(pl.BlockSpec(memory_space=pl.ANY))
    return pl.pallas_call(
        functools.partial(attention_body, order=order, heads=heads, kv_head=kv_head),
        grid=(1,),
        in_specs=specs,
        out_specs=wide,
        out_shape=jax.ShapeDtypeStruct((rows, width), BF16),
        scratch_shapes=[pltpu.VMEM((rows, 2 * side), F32)],
        input_output_aliases=aliases,
        cost_estimate=cost(entries * HD * 4, 4 * rows * heads * HD + 8 * side * HD, entries),
        compiler_params=grant(WIDE),
        name="attention",
    )(*operands)


def fold_rows(table, width):
    rows, narrow = table.shape
    short = rows * narrow // width
    return jnp.concatenate([table[at : at + short] for at in range(0, rows, short)], axis=1)


def unfold_rows(folded, narrow):
    return jnp.concatenate(
        [folded[:, at : at + narrow] for at in range(0, folded.shape[1], narrow)], axis=0
    )


def front_body(*refs):
    sources, (rim_ref, act_ref, part_ref), refs = refs[:5], refs[5:8], refs[8:]
    targets, (low_sum, bc_sum, sems) = refs[:5], refs[5:]
    x_ref, weight_ref, bias_ref, low_ref, bc_ref = targets
    step = pl.program_id(0)
    width = act_ref.shape[1]
    rows = x_ref.shape[0]
    rank = low_ref.shape[1]
    here = pl.ds(pl.multiple_of(step * width, LANES), width)

    def fetches(turn):
        span = pl.ds(pl.multiple_of(turn * width, LANES), width)
        copies = []
        for index, (source, target) in enumerate(zip(sources, targets)):
            at = (span,) if target is low_ref else (slice(None), span)
            copies.append(pltpu.make_async_copy(source.at[at], target.at[at], sems.at[index, turn]))
        return copies

    @pl.when(step == 0)
    def _():
        for turn in range(sems.shape[1]):
            for copy in fetches(turn):
                copy.start()

    for copy in fetches(step):
        copy.wait()

    extended = jnp.concatenate([rim_ref[:, here].astype(F32), x_ref[:, here].astype(F32)], axis=0)
    mixed = bias_ref[:, here]
    for tap in range(CONV):
        start = RIM - (CONV - 1) + tap
        mixed = mixed + weight_ref[tap : tap + 1, here] * extended[start : start + rows, :]
    act = (mixed / (1.0 + jnp.exp(-mixed))).astype(BF16)
    act_ref[...] = act
    low = jnp.dot(act, low_ref[here, :], preferred_element_type=F32)
    bc = lax.dot_general(act, bc_ref[:, here], CONTRACT_LAST, preferred_element_type=F32)

    @pl.when(step == 0)
    def _():
        low_sum[...] = low
        bc_sum[...] = bc

    @pl.when(step > 0)
    def _():
        low_sum[...] += low
        bc_sum[...] += bc

    @pl.when(step == pl.num_programs(0) - 1)
    def _():
        part_ref[:rows, :] = low_sum[...].astype(BF16)
        part_ref[rows:, :] = fold_rows(bc_sum[...], rank).astype(BF16)


def front_call(mamba_in, rim, conv_weight, conv_bias, low_weight, bc_weight):
    rows, channels = mamba_in.shape
    rank, maps = low_weight.shape[1], bc_weight.shape[0]
    tall = rows + rows * maps // rank
    width = min(FRONT_WIDTH, channels)
    fetched = [mamba_in, conv_weight, conv_bias, low_weight, bc_weight]
    return pl.pallas_call(
        front_body,
        grid=(channels // width,),
        in_specs=[pl.BlockSpec(memory_space=pl.ANY)] * len(fetched) + [resident()],
        out_specs=[pl.BlockSpec((rows, width), lambda i: (0, i)), resident()],
        out_shape=[
            jax.ShapeDtypeStruct((rows, channels), BF16),
            jax.ShapeDtypeStruct((tall, rank), BF16),
        ],
        scratch_shapes=[
            *[pltpu.VMEM(array.shape, array.dtype) for array in fetched],
            pltpu.VMEM((rows, rank), F32),
            pltpu.VMEM((rows, maps), F32),
            pltpu.SemaphoreType.DMA((len(fetched), channels // width)),
        ],
        cost_estimate=cost(
            2 * rows * channels * (rank + maps), channels * (4 * rows + 2 * (rank + maps)), rows * channels
        ),
        compiler_params=grant(FRONT_GRANT),
        name="front",
    )(*fetched, rim)


def spread_rows(table, spread):
    rows = table.shape[0]
    tall = rows * STATE
    picker = lax.broadcasted_iota(jnp.int32, (tall, rows), 0) // STATE
    picker = picker == lax.broadcasted_iota(jnp.int32, (tall, rows), 1)
    picked = jnp.dot(picker.astype(F32).astype(BF16), table.astype(BF16), preferred_element_type=F32)
    state = lax.broadcasted_iota(jnp.int32, (tall, STATE), 0) % STATE
    kept = state == lax.broadcasted_iota(jnp.int32, (tall, STATE), 1)
    picked = jnp.where(kept, picked, 0.0).astype(BF16)
    spread[...] = jnp.dot(picked, jnp.ones((STATE, LANES), BF16), preferred_element_type=F32)


def tail_width(channels):
    return max(LANES, channels // STATE)


def sums_of(packed, channels):
    wide = tail_width(channels)
    return jnp.concatenate(
        [packed[row : row + 1, channels : channels + wide] for row in range(channels // wide)], axis=1
    )


def store_sums(ref, row, channels):
    wide = tail_width(channels)
    pieces = [row[:, at : at + wide] for at in range(0, channels, wide)]
    spare = STATE - len(pieces)
    if spare:
        pieces.append(jnp.zeros((spare, wide), F32))
    ref[:, channels:] = jnp.concatenate(pieces, axis=0).astype(BF16)


def advance(states, tiles, rates, step_ref, drive_ref, spread, base, offset, size):
    start = pl.multiple_of(base, size)
    inmap = spread[pl.ds(start * STATE + offset * STATE, STATE), :]
    moved = []
    for tile in range(tiles):
        lanes = pl.ds(tile * LANES, LANES)
        step = step_ref.at[pl.ds(start, size), lanes][pl.ds(offset, 1), :]
        drive = drive_ref.at[pl.ds(start, size), lanes][pl.ds(offset, 1), :]
        moved.append(jnp.exp2(step * rates[:, lanes]) * states[tile] + drive * inmap)
    return moved


def softplus(v):
    return jnp.maximum(v, 0.0) + jnp.log1p(jnp.exp(-jnp.abs(v)))


def rates_of(log_ref):
    return jnp.exp(log_ref[...]) * -LOG2E


def split_lanes(value):
    return [value[:, start : start + LANES] for start in range(0, value.shape[1], LANES)]


def ends_body(
    mine_ref, other_ref, gain_ref, weight_ref, bias_ref, log_ref, act_ref, step_ref, end_ref, bc_ref, normed, spread, drive, sums, rates, wide_step
):
    rows, width = act_ref.shape
    maps = bc_ref.shape[1]
    channels = sums.shape[1]
    tiles = width // LANES
    here = pl.multiple_of(pl.program_id(0) * width, LANES)

    @pl.when(pl.program_id(0) == 0)
    def _():
        both = mine_ref[...].astype(F32) + other_ref[...].astype(F32)
        low = both[:rows]
        scale = lax.rsqrt(jnp.mean(low * low, axis=1, keepdims=True) + 1e-06)
        normed[...] = (low * scale * gain_ref[...]).astype(BF16)
        bc = unfold_rows(both[rows:], maps)
        bc_ref[...] = bc
        spread_rows(bc[:, :STATE], spread)

    step = softplus(
        jnp.dot(normed[...], weight_ref[...], preferred_element_type=F32) + bias_ref[...]
    )
    wide_step[...] = step
    step_ref[...] = step.astype(BF16)
    drive[...] = step * act_ref[...].astype(F32)
    sums[:, pl.ds(here, width)] = jnp.sum(step, axis=0, keepdims=True)
    rates[...] = rates_of(log_ref)

    def block(index, states):
        states = list(states)
        for offset in range(END_BLOCK):
            states = advance(
                states, tiles, rates, wide_step, drive, spread, index * END_BLOCK, offset, END_BLOCK
            )
        return tuple(states)

    states = lax.fori_loop(
        0, rows // END_BLOCK, block, tuple(jnp.zeros((STATE, LANES), F32) for _ in range(tiles))
    )
    for tile in range(tiles):
        lanes = pl.ds(pl.multiple_of(here + tile * LANES, LANES), LANES)
        end_ref[:, lanes] = states[tile].astype(BF16)

    @pl.when(pl.program_id(0) == pl.num_programs(0) - 1)
    def _():
        store_sums(end_ref, sums[...], channels)


def ends_call(mine, other, low_gain, dt_weight, dt_bias, rate_log, act):
    rows, channels = act.shape
    tall, rank = mine.shape
    maps = (tall - rows) * rank // rows
    width = min(1024, channels)
    block = lambda height: pl.BlockSpec((height, width), lambda i: (0, i))
    whole = lambda shape: pl.BlockSpec(shape, lambda i: (0, 0))
    packed = (STATE, channels + tail_width(channels))
    return pl.pallas_call(
        ends_body,
        grid=(channels // width,),
        in_specs=[
            resident(),
            resident(),
            whole((1, rank)),
            block(rank),
            block(1),
            block(STATE),
            block(rows),
        ],
        out_specs=[block(rows), resident(), whole((rows, maps))],
        out_shape=[
            jax.ShapeDtypeStruct((rows, channels), BF16),
            jax.ShapeDtypeStruct(packed, BF16),
            jax.ShapeDtypeStruct((rows, maps), F32),
        ],
        scratch_shapes=[
            pltpu.VMEM((rows, rank), BF16),
            pltpu.VMEM((rows * STATE, LANES), F32),
            pltpu.VMEM((rows, width), F32),
            pltpu.VMEM((1, channels), F32),
            pltpu.VMEM((STATE, width), F32),
            pltpu.VMEM((rows, width), F32),
        ],
        cost_estimate=cost(
            channels * rows * (2 * rank + 4 * STATE), channels * (6 * rows + 2 * rank), rows * channels * STATE
        ),
        compiler_params=grant(WIDE),
        name="ends",
    )(mine, other, low_gain, dt_weight, dt_bias, rate_log, act)


def join_body(place, own_ref, got_ref, log_ref, out_ref, *, step):
    channels = log_ref.shape[1]
    upper = (place[0] & step) != 0
    own = own_ref[...].astype(F32)
    got = got_ref[...].astype(F32)
    early = jnp.where(upper, got, own)
    late = jnp.where(upper, own, got)
    decay = jnp.exp2(rates_of(log_ref) * sums_of(late, channels))
    out_ref[:, :channels] = (early[:, :channels] * decay + late[:, :channels]).astype(BF16)
    out_ref[:, channels:] = (early[:, channels:] + late[:, channels:]).astype(BF16)


def join_call(place, own, got, rate_log, step):
    return pl.pallas_call(
        functools.partial(join_body, step=step),
        in_specs=[pl.BlockSpec(memory_space=pltpu.SMEM), resident(), resident(), resident()],
        out_specs=resident(),
        out_shape=jax.ShapeDtypeStruct(own.shape, BF16),
        cost_estimate=cost(8 * own.size, 10 * own.size, own.size),
        compiler_params=grant(16),
        name="join",
    )(place, own, got, rate_log)


def scan_body(place, *refs, steps):
    got_refs, refs = refs[: len(steps)], refs[len(steps) :]
    step_ref, act_ref, gate_ref, bc_ref, log_ref, skip_ref, out_ref = refs[:7]
    spread, outmap, drive, enter, rates, wide_step, even, odd = refs[7:]
    rows, width = act_ref.shape
    tiles = width // LANES
    channels = enter.shape[1]
    deep = TOKEN_BLOCK * STATE
    here = pl.multiple_of(pl.program_id(0) * width, LANES)

    @pl.when(pl.program_id(0) == 0)
    def _():
        every = rates_of(log_ref)
        state = jnp.zeros((STATE, channels), F32)
        passed = jnp.zeros((1, channels), F32)
        for step, got_ref in zip(steps, got_refs):
            upper = (place[0] & step) != 0
            got = got_ref[...].astype(F32)
            state = jnp.where(upper, got[:, :channels] * jnp.exp2(every * passed) + state, state)
            passed = jnp.where(upper, sums_of(got, channels) + passed, passed)
        enter[...] = state

        spread_rows(bc_ref[:, :STATE], spread)
        place_in = lax.broadcasted_iota(jnp.int32, (STATE, deep), 1)
        repeat = (place_in % STATE) == lax.broadcasted_iota(jnp.int32, (STATE, deep), 0)
        wide = jnp.dot(
            bc_ref[:, STATE:].astype(BF16), repeat.astype(F32).astype(BF16), preferred_element_type=F32
        )
        token = lax.broadcasted_iota(jnp.int32, (rows, deep), 0) % TOKEN_BLOCK
        own = token == lax.broadcasted_iota(jnp.int32, (rows, deep), 1) // STATE
        outmap[...] = jnp.where(own, wide, 0.0).astype(BF16)

    wide_step[...] = step_ref[...].astype(F32)
    drive[...] = wide_step[...] * act_ref[...].astype(F32)
    rates[...] = jnp.exp(log_ref[:, pl.ds(here, width)]) * -LOG2E

    def walk(index, states, held):
        states = list(states)
        for offset in range(TOKEN_BLOCK):
            states = advance(
                states, tiles, rates, wide_step, drive, spread, index * TOKEN_BLOCK, offset, TOKEN_BLOCK
            )
            for tile in range(tiles):
                held[offset * STATE : (offset + 1) * STATE, tile * LANES : (tile + 1) * LANES] = states[tile]
        return tuple(states)

    def emit(index, held):
        span = pl.ds(pl.multiple_of(index * TOKEN_BLOCK, TOKEN_BLOCK), TOKEN_BLOCK)
        summed = jnp.dot(outmap[span, :], held[...].astype(BF16), preferred_element_type=F32)
        summed = summed + skip_ref[...] * act_ref[span, :].astype(F32)
        gate = gate_ref[span, :].astype(F32)
        out_ref[span, :] = (summed * (gate / (1.0 + jnp.exp(-gate)))).astype(BF16)

    def pair(index, states):
        states = walk(2 * index + 1, states, odd)
        emit(2 * index, even)
        states = walk(2 * index + 2, states, even)
        emit(2 * index + 1, odd)
        return states

    blocks = rows // TOKEN_BLOCK
    states = walk(0, split_lanes(enter[:, pl.ds(here, width)]), even)
    states = lax.fori_loop(0, blocks // 2 - 1, pair, states)
    walk(blocks - 1, states, odd)
    emit(blocks - 2, even)
    emit(blocks - 1, odd)


def scan_call(place, gots, step, act, gate, bc, rate_log, skip):
    rows, channels = act.shape
    width = min(1024, channels)
    block = lambda height: pl.BlockSpec((height, width), lambda i: (0, i))
    whole = lambda shape: pl.BlockSpec(shape, lambda i: (0, 0))
    deep = TOKEN_BLOCK * STATE
    return pl.pallas_call(
        functools.partial(scan_body, steps=bits_of(2 ** len(gots))),
        grid=(channels // width,),
        in_specs=[
            pl.BlockSpec(memory_space=pltpu.SMEM),
            *[resident() for got in gots],
            block(rows),
            block(rows),
            block(rows),
            whole(bc.shape),
            whole(rate_log.shape),
            block(1),
        ],
        out_specs=block(rows),
        out_shape=jax.ShapeDtypeStruct((rows, channels), BF16),
        scratch_shapes=[
            pltpu.VMEM((rows * STATE, LANES), F32),
            pltpu.VMEM((rows, deep), BF16),
            pltpu.VMEM((rows, width), F32),
            pltpu.VMEM((STATE, channels), F32),
            pltpu.VMEM((STATE, width), F32),
            pltpu.VMEM((rows, width), F32),
            pltpu.VMEM((deep, width), F32),
            pltpu.VMEM((deep, width), F32),
        ],
        cost_estimate=cost(8 * channels * rows * STATE, channels * rows * 10, rows * channels * STATE),
        compiler_params=grant(WIDE),
        name="scan",
    )(place, *gots, step, act, gate, bc, rate_log, skip)


def per_device(
    queries,
    key_heads,
    value_heads,
    span_order,
    block_mask,
    mamba_in,
    gate_in,
    conv_weight,
    conv_bias,
    low_weight,
    bc_weight,
    low_gain,
    dt_weight,
    dt_bias,
    rate_log,
    skip_gain,
):
    row_count = queries.shape[0]
    count = lax.axis_size("ctx")
    head_devices = lax.axis_size("head")
    place = lax.axis_index("ctx").astype(jnp.int32)[None]

    tail, key_heads, value_heads = after((mamba_in[row_count - RIM :], key_heads, value_heads))
    rim = lax.ppermute(tail, "ctx", [(i, i + 1) for i in range(count - 1)])

    kv_count = key_heads.shape[1] // HD
    local_kv = max(1, kv_count // head_devices)
    query_local = queries.shape[1] // HD
    group_size = query_local * head_devices // kv_count
    kv_start = lax.axis_index("head") * query_local // group_size
    near = jnp.concatenate(
        [
            lax.dynamic_slice_in_dim(key_heads, kv_start * HD, local_kv * HD, 1),
            lax.dynamic_slice_in_dim(value_heads, kv_start * HD, local_kv * HD, 1),
        ],
        axis=1,
    )
    kv_hops = bits_of(count)[::-1]
    kv_hops[:2] = kv_hops[:2][::-1]
    order = [0]
    for hop in kv_hops:
        order = order + [flip ^ hop for flip in order]
    far = swap(near, "ctx", kv_hops[0])

    def gather_on(near, far, turn):
        near = jnp.concatenate([near, far], axis=0)
        return near, swap(near, "ctx", kv_hops[turn])

    logs = rate_log.T
    if len(kv_hops) > 1:
        near, far = gather_on(near, far, 1)
        rim, near = after((rim, near))
    act, part = front_call(mamba_in, rim, conv_weight, conv_bias[None, :], low_weight, bc_weight.T)
    hops = bits_of(head_devices)
    for hop in hops:
        other = swap(part, "head", hop)
        if hop != hops[-1]:
            part = (part.astype(F32) + other.astype(F32)).astype(BF16)
    for turn in range(2, len(kv_hops)):
        near, far = gather_on(near, far, turn)
    step_dt, packed, bc = ends_call(
        part, other, low_gain[None, :], dt_weight, dt_bias[None, :], logs, act
    )

    attn_out = None
    gots = []
    hops = bits_of(count)
    halves = 2 if query_local // local_kv % 2 == 0 else 1
    pieces = [(run, local_kv * halves) for run in range(local_kv * halves)]
    if local_kv > 1 and halves == 2:
        pieces = [(0, local_kv)] + pieces[2:]
    for turn, hop in enumerate(hops):
        if 2 * hop == count:
            pairs = [(i, i ^ hop) for i in range(count) if not i & hop]
            got = lax.ppermute(packed, "ctx", pairs)
        else:
            got = swap(packed, "ctx", hop)
        for run, runs in pieces[turn : turn + 1] if 2 * hop < count else pieces[turn:]:
            packed, queries, near, attn_out = after((packed, queries, near, attn_out))
            attn_out = attention_call(
                place, span_order, block_mask, queries, near, far, attn_out, run, runs, tuple(order)
            )
        got, attn_out = after((got, attn_out))
        if 2 * hop < count:
            packed = join_call(place, packed, got, logs, hop)
        gots.append(got)
    mamba_out = scan_call(place, gots, step_dt, act, gate_in, bc, logs, skip_gain[None, :])
    return (attn_out, mamba_out)


def solution(mesh):
    in_specs = (
        P("ctx", "head"),
        P("ctx", None),
        P("ctx", None),
        P(),
        P(),
        P("ctx", "head"),
        P("ctx", "head"),
        P(None, "head"),
        P("head"),
        P("head", None),
        P("head", None),
        P(),
        P(None, "head"),
        P("head"),
        P("head", None),
        P("head"),
    )
    out_specs = (P("ctx", "head"), P("ctx", "head"))

    return jax.shard_map(
        per_device, mesh=mesh, in_specs=in_specs, out_specs=out_specs, check_vma=False
    )
```
